32 devices in a mesh: video: 4 (over x, core), frame: 8 (over z, y).
Axes of the slice: x: 2, y: 2, z: 4, core: 2. Of those that a mesh axis runs over, the one named last changes fastest.
Arguments:
- frames: bfloat16 [32, 1024, 640], P(('video', 'frame')), parts along dimension 0, may hold values from -6 to 6
- ref_rows: bfloat16 [4096, 640], P(('video', 'frame')), parts along dimension 0, may hold values from -6 to 6
- w_query: bfloat16 [640, 640], replicated, may hold values from -1 to 1
- w_key: bfloat16 [640, 640], replicated, may hold values from -1 to 1
- w_value: bfloat16 [640, 640], replicated, may hold values from -0.25 to 0.25
- w_out: bfloat16 [640, 640], replicated, may hold values from -0.25 to 0.25
- w_conv: bfloat16 [3, 640, 640], replicated, may hold values from -0.125 to 0.125
- t_query: bfloat16 [640, 640], replicated, may hold values from -1 to 1
- t_key: bfloat16 [640, 640], replicated, may hold values from -1 to 1
- t_value: bfloat16 [640, 640], replicated, may hold values from -0.25 to 0.25
- t_out: bfloat16 [640, 640], replicated, may hold values from -0.25 to 0.25
Outputs:
- result: bfloat16 [32, 1024, 640], P(('video', 'frame')), parts along dimension 0
The draws below stay inside these ranges and needn't reach their ends.
There are 4 independent parts, one for each index of `video`. The reference program is written for one: setup_inputs(seed, part) draws one part's arguments, and reference() takes and returns one part's arrays. A program takes and returns all parts, laid end to end along the dimension named above; an argument that names none is the same for every part. Nothing has to cross between parts.
All inputs are finite; a program needn't handle non-finite values.
Results may differ from the reference program's by a relative error of at most 0.011.
Values may be sent and summed in bfloat16 or wider, within the bound.
A program may use at most 128 MiB of HBM per device.

```python
import math
import jax
import jax.numpy as jnp
from jax import lax

C = 640
HEADS = 10
HW = 1024
FRAMES = 8


def own_part(key, tag):
    return jax.random.normal(jax.random.fold_in(key, tag), (C, C), jnp.float32)


def draw_w_query(key, part):
    value = own_part(key, 21) / math.sqrt(C)
    return jnp.clip(value, -1.0, 1.0).astype(jnp.bfloat16)


def draw_w_key(key, part):
    value = own_part(key, 22) / math.sqrt(C)
    return jnp.clip(value, -1.0, 1.0).astype(jnp.bfloat16)


def draw_t_query(key, part):
    value = own_part(key, 23) / math.sqrt(C)
    return jnp.clip(value, -1.0, 1.0).astype(jnp.bfloat16)


def draw_t_key(key, part):
    value = own_part(key, 24) / math.sqrt(C)
    return jnp.clip(value, -1.0, 1.0).astype(jnp.bfloat16)


def shard_levels(stream_key, extent, shards, least, largest):
    factor_of, own = 1.0, jax.random.fold_in(stream_key, 6)
    for axis_at, blocks in shards:
        heights = jnp.exp(jax.random.uniform(jax.random.fold_in(own, axis_at), (blocks,), jnp.float32, least / len(shards), largest / len(shards)))
        factor_of = factor_of * jnp.repeat(heights, extent[axis_at] // blocks).reshape([-1 if axis == axis_at else 1 for axis in range(len(extent))])
    return factor_of


def centred(key, shape, scale, reach, pieces=(), dtype=jnp.bfloat16):
    entries = jax.random.normal(key, shape, jnp.float32) * scale
    if len(pieces) > 0:
        entries = shard_levels(key, shape, pieces, -0.22, 0.18) * entries
    return jnp.clip(entries, min=-reach, max=reach).astype(dtype)


def setup_inputs(seed: int = 0, part: int = 0) -> dict:
    arg_keys = jax.random.split(jax.random.key(seed), 12)
    part_splits = jax.random.split(jax.random.fold_in(arg_keys[11], part), 12)
    frames = centred(part_splits[0], (FRAMES, HW, C), 1.0, 6.0, ((0, 8),))
    ref_rows = centred(part_splits[1], (HW, C), 1.0, 6.0, ((0, 8),))
    w_query = draw_w_query(jax.random.fold_in(arg_keys[11], 71), part)
    w_key = draw_w_key(jax.random.fold_in(arg_keys[11], 71), part)
    w_value = centred(arg_keys[4], (C, C), C ** -0.5, 0.25)
    w_out = centred(arg_keys[5], (C, C), C ** -0.5, 0.25)
    w_conv = centred(arg_keys[6], (3, C, C), (3 * C) ** -0.5, 0.125)
    t_query = draw_t_query(jax.random.fold_in(arg_keys[11], 71), part)
    t_key = draw_t_key(jax.random.fold_in(arg_keys[11], 71), part)
    t_value = centred(arg_keys[9], (C, C), C ** -0.5, 0.25)
    t_out = centred(arg_keys[10], (C, C), C ** -0.5, 0.25)
    return dict(frames=frames, ref_rows=ref_rows, w_query=w_query, w_key=w_key, w_value=w_value, w_out=w_out, w_conv=w_conv, t_query=t_query, t_key=t_key, t_value=t_value, t_out=t_out)


def rounded(value):
    return lax.optimization_barrier(value.astype(jnp.bfloat16)).astype(jnp.float32)

def layer_norm(value):
    mean = lax.optimization_barrier(jnp.mean(value, axis=-1, keepdims=True))
    centered = value - mean
    var = lax.optimization_barrier(jnp.mean(centered * centered, axis=-1, keepdims=True))
    return centered * lax.rsqrt(var + 1e-05)

def project(rows, weight):
    return jnp.dot(rows, weight, preferred_element_type=jnp.float32).astype(jnp.bfloat16)

def reference(frames, ref_rows, w_query, w_key, w_value, w_out, w_conv, t_query, t_key, t_value, t_out):
    nframes, pixels, width = frames.shape
    head_dim = width // HEADS
    scale = 1.0 / math.sqrt(head_dim)
    normed = layer_norm(frames.astype(jnp.float32)).astype(jnp.bfloat16).reshape(-1, width)
    query = project(normed, w_query).astype(jnp.float32).reshape(nframes, pixels, HEADS, head_dim)
    keys = project(normed, w_key).astype(jnp.float32).reshape(nframes, pixels, HEADS, head_dim)
    values = project(normed, w_value).astype(jnp.float32).reshape(nframes, pixels, HEADS, head_dim)
    ref_keys = project(ref_rows, w_key).astype(jnp.float32).reshape(pixels, HEADS, head_dim)
    ref_values = project(ref_rows, w_value).astype(jnp.float32).reshape(pixels, HEADS, head_dim)

    def one_head(args):
        qa, ka, va, rka, rva = args
        own = jnp.einsum('fqd,fkd->fqk', qa, ka) * scale
        far = jnp.einsum('fqd,kd->fqk', qa, rka) * scale
        scores = jnp.concatenate([own, far], axis=-1)
        peak = lax.optimization_barrier(jnp.max(scores, axis=-1, keepdims=True))
        expo = jnp.exp(scores - peak)
        total = lax.optimization_barrier(jnp.sum(expo, axis=-1))
        weights = rounded(expo)
        mixed = jnp.einsum('fqk,fkd->fqd', weights[:, :, :pixels], va)
        mixed = mixed + jnp.einsum('fqk,kd->fqd', weights[:, :, pixels:], rva)
        return mixed / total[..., None]
    per_head = lax.map(one_head, (query.transpose(2, 0, 1, 3), keys.transpose(2, 0, 1, 3), values.transpose(2, 0, 1, 3), ref_keys.transpose(1, 0, 2), ref_values.transpose(1, 0, 2)))
    attended = per_head.transpose(1, 2, 0, 3).reshape(-1, width).astype(jnp.bfloat16)
    first = (frames.astype(jnp.float32) + jnp.dot(attended, w_out, preferred_element_type=jnp.float32).reshape(nframes, pixels, width)).astype(jnp.bfloat16)
    padded = jnp.pad(first, ((1, 1), (0, 0), (0, 0)))
    conv = jnp.zeros((nframes * pixels, width), jnp.float32)
    for tap in range(3):
        conv = conv + jnp.dot(padded[tap:tap + nframes].reshape(-1, width), w_conv[tap], preferred_element_type=jnp.float32)
    second = (first.astype(jnp.float32) + conv.reshape(nframes, pixels, width)).astype(jnp.bfloat16)
    normed2 = layer_norm(second.astype(jnp.float32)).astype(jnp.bfloat16).reshape(-1, width)
    tquery = project(normed2, t_query).astype(jnp.float32).reshape(nframes, pixels, HEADS, head_dim)
    tkeys = project(normed2, t_key).astype(jnp.float32).reshape(nframes, pixels, HEADS, head_dim)
    tvalues = project(normed2, t_value).astype(jnp.float32).reshape(nframes, pixels, HEADS, head_dim)
    tscores = jnp.einsum('fnhd,gnhd->nhfg', tquery, tkeys) * scale
    tpeak = lax.optimization_barrier(jnp.max(tscores, axis=-1, keepdims=True))
    texpo = jnp.exp(tscores - tpeak)
    ttotal = lax.optimization_barrier(jnp.sum(texpo, axis=-1))
    tmixed = jnp.einsum('nhfg,gnhd->nhfd', rounded(texpo), tvalues) / ttotal[..., None]
    tattended = tmixed.transpose(2, 0, 1, 3).reshape(-1, width).astype(jnp.bfloat16)
    result = second.astype(jnp.float32) + jnp.dot(tattended, t_out, preferred_element_type=jnp.float32).reshape(nframes, pixels, width)
    return result.astype(jnp.bfloat16)
```

```python
import functools
import math

import jax
import jax.numpy as jnp
from jax import lax
from jax.experimental import pallas as pl
from jax.experimental.pallas import tpu as pltpu
from jax.sharding import PartitionSpec as P

HEADS = 10
F32 = jnp.float32
BF16 = jnp.bfloat16
LOG2E = math.log2(math.e)
SIZE = 16
LAG = 3
MESH = pl.DeviceIdType.MESH


def layer_norm(value):
    mean = jnp.mean(value, axis=-1, keepdims=True)
    centered = value - mean
    var = jnp.mean(centered * centered, axis=-1, keepdims=True)
    return centered * lax.rsqrt(var + 1e-05)


def dot(a, b):
    return jnp.dot(a, b, preferred_element_type=F32)


def dot_nt(a, b):
    return lax.dot_general(a, b, (((1,), (1,)), ((), ())), preferred_element_type=F32)


def remote(src, dst, send, recv, device):
    return pltpu.make_async_remote_copy(
        src_ref=src,
        dst_ref=dst,
        send_sem=send,
        recv_sem=recv,
        device_id={"frame": device},
        device_id_type=MESH,
    )


def split_heads(low, rows):
    zero = jnp.zeros_like(rows)
    return jnp.concatenate([jnp.where(low, rows, zero), jnp.where(low, zero, rows)], axis=0)


def kernel(
    ndev,
    x_hbm,
    ref_hbm,
    wq_hbm,
    wk_hbm,
    wv_hbm,
    wo_hbm,
    wc_hbm,
    tq_hbm,
    tk_hbm,
    tv_hbm,
    to_hbm,
    out_ref,
    xbuf,
    wqkv,
    wo,
    wc,
    tqkv,
    to,
    refbuf,
    qbuf,
    kbuf,
    vbuf,
    abuf,
    fbuf,
    rbuf,
    tab,
    resbuf,
    x_sem,
    w_sem,
    up_send,
    down_send,
    side_send,
    ref_recv,
    there_send,
    there_recv,
    back_send,
    back_recv,
):
    group, width = xbuf.shape[1:]
    pixels = ndev * group
    pairs = HEADS // 2
    head_dim = width // HEADS
    qscale = LOG2E / math.sqrt(head_dim)
    chunks = fbuf.shape[0]
    size = group // chunks
    block = ndev * size
    line = ndev // 2
    me = lax.axis_index("frame")
    side = lax.rem(me, 2)
    place = me // 2
    partner = me + 1 - 2 * side

    barrier = pltpu.get_barrier_semaphore()
    for off in range(1, ndev):
        pl.semaphore_signal(
            barrier,
            inc=1,
            device_id={"frame": lax.rem(me + off, ndev)},
            device_id_type=MESH,
        )

    def columns(index):
        return pl.ds(index * width, width)

    steps = ndev // 2
    own_load = pltpu.make_async_copy(ref_hbm, refbuf.at[me], ref_recv.at[me])
    x_loads = [
        pltpu.make_async_copy(
            x_hbm.at[pl.ds(2 * step, 2)], xbuf.at[pl.ds(2 * step, 2)], x_sem.at[step]
        )
        for step in range(steps)
    ]
    places = [
        (wq_hbm, wqkv.at[:, columns(0)]),
        (wk_hbm, wqkv.at[:, columns(1)]),
        (wv_hbm, wqkv.at[:, columns(2)]),
        (wo_hbm, wo),
        (wc_hbm, wc),
        (tq_hbm, tqkv.at[:, columns(0)]),
        (tk_hbm, tqkv.at[:, columns(1)]),
        (tv_hbm, tqkv.at[:, columns(2)]),
        (to_hbm, to),
    ]
    w_loads = [
        pltpu.make_async_copy(src, dst, w_sem.at[index]) for index, (src, dst) in enumerate(places)
    ]
    own_load.start()
    x_loads[0].start()
    for load in w_loads[:3]:
        load.start()
    for load in x_loads[1:]:
        load.start()
    for load in w_loads[3:]:
        load.start()

    own_load.wait()
    pl.semaphore_wait(barrier, ndev - 1)

    def up_copy(owner, step):
        return remote(
            refbuf.at[owner], refbuf.at[owner], up_send.at[step], ref_recv.at[owner], me + 2
        )

    def down_copy(owner, step):
        return remote(
            refbuf.at[owner], refbuf.at[owner], down_send.at[step], ref_recv.at[owner], me - 2
        )

    def side_copy(owner, slot):
        return remote(
            refbuf.at[owner], refbuf.at[owner], side_send.at[slot], ref_recv.at[owner], partner
        )

    @pl.when(place < line - 1)
    def _():
        up_copy(me, 0).start()

    @pl.when(place > 0)
    def _():
        down_copy(me, 0).start()

    side_copy(me, 0).start()

    def from_below(step, body):
        @pl.when(place - 1 - step >= 0)
        def _():
            body(me - 2 * (step + 1))

    def from_above(step, body):
        @pl.when(place + 1 + step <= line - 1)
        def _():
            body(me + 2 * (step + 1))

    def hand_on(step):
        def lower(owner):
            side_copy(owner, 1 + 2 * step).wait_recv()
            if step < line - 2:

                @pl.when(place < line - 1)
                def _():
                    up_copy(owner, step + 1).start()

            side_copy(owner, 1 + 2 * step).start()

        def upper(owner):
            side_copy(owner, 2 + 2 * step).wait_recv()
            if step < line - 2:

                @pl.when(place > 0)
                def _():
                    down_copy(owner, step + 1).start()

            side_copy(owner, 2 + 2 * step).start()

        from_below(step, lower)
        from_above(step, upper)

    def own_rows(step):
        x_loads[step].wait()
        rows = pl.ds(step * 2 * group, 2 * group)
        both = pl.ds(step * 2, 2)
        x = xbuf[both].reshape(2 * group, width)
        normed = layer_norm(x.astype(F32)).astype(BF16)
        projected = dot(normed, wqkv[...])
        qbuf[both] = (projected[:, :width] * qscale).astype(BF16).reshape(2, group, width)
        kbuf[rows, :] = projected[:, width : 2 * width].astype(BF16)
        values = projected[:, 2 * width :].astype(BF16)
        for pair in range(pairs):
            vbuf[pair, rows, 0:128] = values[:, pair * 128 : pair * 128 + 128]
            vbuf[pair, rows, 128:256] = jnp.ones((2 * group, 128), BF16)

    def ref_project(owner):
        rows = pl.ds(pl.multiple_of(pixels + owner * group, group), group)
        projected = dot(refbuf[owner], wqkv[:, width:])
        kbuf[rows, :] = projected[:, :width].astype(BF16)
        values = projected[:, width:].astype(BF16)
        for pair in range(pairs):
            vbuf[pair, rows, 0:128] = values[:, pair * 128 : pair * 128 + 128]
            vbuf[pair, rows, 128:256] = jnp.ones((group, 128), BF16)

    for load in w_loads[:3]:
        load.wait()
    handed = 0
    for step in range(steps):
        own_rows(step)
        if step >= steps - 2 and handed < line - 1:
            hand_on(handed)
            handed += 1
    ref_project(me)
    for step in range(line - 1):
        if step >= handed:
            hand_on(step)
        from_below(step, ref_project)
        from_above(step, ref_project)

    def beside(owner):
        side_copy(owner, 0).wait_recv()
        ref_project(owner)

    beside(partner)
    for step in range(line - 1):
        from_below(step, lambda owner: beside(owner + partner - me))
        from_above(step, lambda owner: beside(owner + partner - me))

    low = lax.broadcasted_iota(jnp.int32, (block, 128), 1) < 64

    def there_copy(chunk, target, sender):
        return remote(
            fbuf.at[chunk, target],
            rbuf.at[chunk, sender],
            there_send.at[chunk * ndev + target],
            there_recv.at[chunk * ndev + sender],
            target,
        )

    def back_copy(chunk, target, sender):
        return remote(
            resbuf.at[chunk, target],
            out_ref.at[pl.ds(pl.multiple_of(sender * group + chunk * size, size), size)],
            back_send.at[chunk * ndev + target],
            back_recv.at[chunk * ndev + sender],
            target,
        )

    def attend(chunk):
        rows = pl.ds(pl.multiple_of(chunk * size, size), size)

        for pair in range(pairs):
            lanes = pl.ds(pair * 128, 128)
            queries = split_heads(low, qbuf[:, rows, lanes].reshape(block, 128))
            scores = dot_nt(queries, kbuf[:, lanes])
            peak = jnp.max(scores, axis=-1, keepdims=True)
            expo = jnp.exp2(scores - peak).astype(BF16)
            both = dot(expo, vbuf[pair])
            mixed = both[:, :128] / both[:, 128:]
            abuf[:, lanes] = jnp.where(low, mixed[:block], mixed[block:]).astype(BF16)

        x = xbuf[:, rows, :].reshape(block, width).astype(F32)
        first = (x + dot(abuf[...], wo[...])).astype(BF16)
        fbuf[chunk] = first.reshape(ndev, size, width)
        for off in reversed(range(1, ndev)):
            there_copy(chunk, lax.rem(me + off, ndev), me).start()
        rbuf[chunk, me] = fbuf[chunk, me]

    same = lax.rem(lax.broadcasted_iota(jnp.int32, (2 * block, block), 0), size) == lax.rem(
        lax.broadcasted_iota(jnp.int32, (2 * block, block), 1), size
    )

    def temporal(chunk):
        for off in range(1, ndev):
            other = lax.rem(me + off, ndev)
            there_copy(chunk, other, other).wait_recv()
        x = rbuf[chunk].reshape(block, width)
        edge = jnp.zeros((size, width), BF16)
        before = jnp.concatenate([edge, x[:-size]], axis=0)
        after = jnp.concatenate([x[size:], edge], axis=0)
        conv = dot(jnp.concatenate([before, x, after], axis=1), wc[...])
        second = (x.astype(F32) + conv).astype(BF16)
        normed = layer_norm(second.astype(F32)).astype(BF16)
        projected = dot(normed, tqkv[...])
        queries = (projected[:, :width] * qscale).astype(BF16)
        keys = projected[:, width : 2 * width].astype(BF16)
        values = projected[:, 2 * width :].astype(BF16)
        ones = jnp.ones((block, 128), BF16)
        for pair in range(pairs):
            lanes = slice(pair * 128, pair * 128 + 128)
            scores = dot_nt(split_heads(low, queries[:, lanes]), keys[:, lanes])
            scores = jnp.where(same, scores, -1e30)
            peak = jnp.max(scores, axis=-1, keepdims=True)
            expo = jnp.exp2(scores - peak).astype(BF16)
            both = dot(expo, jnp.concatenate([values[:, lanes], ones], axis=1))
            mixed = both[:, :128] / both[:, 128:]
            tab[:, lanes] = jnp.where(low, mixed[:block], mixed[block:]).astype(BF16)
        result = second.astype(F32) + dot(tab[...], to[...])
        resbuf[chunk] = result.astype(BF16).reshape(ndev, size, width)
        for off in reversed(range(1, ndev)):
            back_copy(chunk, lax.rem(me + off, ndev), me).start()
        out_ref[pl.ds(pl.multiple_of(me * group + chunk * size, size), size), :] = resbuf[chunk, me]

    for load in w_loads[3:]:
        load.wait()

    def stage(step, carry):
        @pl.when(step < chunks)
        def _():
            attend(step)

        @pl.when(step >= LAG)
        def _():
            temporal(step - LAG)

        return carry

    lax.fori_loop(0, chunks + LAG, stage, 0)

    side_copy(me, 0).wait_send()
    for step in range(line - 1):

        @pl.when(place < line - 1)
        def _():
            if step == 0:
                up_copy(me, 0).wait_send()
            else:
                from_below(step - 1, lambda owner: up_copy(owner, step).wait_send())

        @pl.when(place > 0)
        def _():
            if step == 0:
                down_copy(me, 0).wait_send()
            else:
                from_above(step - 1, lambda owner: down_copy(owner, step).wait_send())

        from_below(step, lambda owner: side_copy(owner, 1 + 2 * step).wait_send())
        from_above(step, lambda owner: side_copy(owner, 2 + 2 * step).wait_send())

    for chunk in range(chunks):
        for off in range(1, ndev):
            other = lax.rem(me + off, ndev)
            there_copy(chunk, other, me).wait_send()
            back_copy(chunk, other, me).wait_send()
            back_copy(chunk, other, other).wait_recv()


def per_device(
    frames, ref_rows, w_query, w_key, w_value, w_out, w_conv, t_query, t_key, t_value, t_out
):
    fdev, pixels, width = frames.shape
    ndev = lax.axis_size("frame")
    group = pixels // ndev
    pairs = HEADS // 2
    chunks = group // SIZE
    block = ndev * SIZE
    line = ndev // 2
    DMA = pltpu.SemaphoreType.DMA
    out = pl.pallas_call(
        functools.partial(kernel, ndev),
        out_shape=pltpu.VMEM((pixels, width), BF16),
        in_specs=[pl.BlockSpec(memory_space=pl.ANY)] * 11,
        out_specs=pl.BlockSpec(memory_space=pltpu.VMEM),
        scratch_shapes=[
            pltpu.VMEM((ndev, group, width), BF16),
            pltpu.VMEM((width, 3 * width), BF16),
            pltpu.VMEM((width, width), BF16),
            pltpu.VMEM((3 * width, width), BF16),
            pltpu.VMEM((width, 3 * width), BF16),
            pltpu.VMEM((width, width), BF16),
            pltpu.VMEM((ndev, group, width), BF16),
            pltpu.VMEM((ndev, group, width), BF16),
            pltpu.VMEM((2 * pixels, width), BF16),
            pltpu.VMEM((pairs, 2 * pixels, 256), BF16),
            pltpu.VMEM((block, width), BF16),
            pltpu.VMEM((chunks, ndev, SIZE, width), BF16),
            pltpu.VMEM((chunks, ndev, SIZE, width), BF16),
            pltpu.VMEM((block, width), BF16),
            pltpu.VMEM((chunks, ndev, SIZE, width), BF16),
            DMA((line,)),
            DMA((9,)),
            DMA((line,)),
            DMA((line,)),
            DMA((ndev,)),
            DMA((ndev,)),
            DMA((chunks * ndev,)),
            DMA((chunks * ndev,)),
            DMA((chunks * ndev,)),
            DMA((chunks * ndev,)),
        ],
        compiler_params=pltpu.CompilerParams(
            collective_id=0, has_side_effects=True, vmem_limit_bytes=56 * 1024 * 1024
        ),
    )(
        frames.reshape(ndev, group, width),
        ref_rows,
        w_query,
        w_key,
        w_value,
        w_out,
        w_conv.reshape(3 * width, width),
        t_query,
        t_key,
        t_value,
        t_out,
    )
    return out.reshape(fdev, pixels, width)


def solution(mesh):
    return jax.shard_map(
        per_device,
        mesh=mesh,
        in_specs=(
            P(("video", "frame"), None, None),
            P(("video", "frame"), None),
            P(),
            P(),
            P(),
            P(),
            P(),
            P(),
            P(),
            P(),
            P(),
        ),
        out_specs=P(("video", "frame"), None, None),
        check_vma=False,
    )
```

```python
import functools
import math

import jax
import jax.numpy as jnp
from jax import lax
from jax.experimental import pallas as pl
from jax.experimental.pallas import tpu as pltpu
from jax.sharding import PartitionSpec as P

HEADS = 10
F32 = jnp.float32
BF16 = jnp.bfloat16
LOG2E = math.log2(math.e)
SIZE = 16
LAG = 3
PARTS = 2
MESH = pl.DeviceIdType.MESH


def layer_norm(value):
    mean = jnp.mean(value, axis=-1, keepdims=True)
    centered = value - mean
    var = jnp.mean(centered * centered, axis=-1, keepdims=True)
    return centered * lax.rsqrt(var + 1e-05)


def dot(a, b):
    return jnp.dot(a, b, preferred_element_type=F32)


def dot_nt(a, b):
    return lax.dot_general(a, b, (((1,), (1,)), ((), ())), preferred_element_type=F32)


def remote(src, dst, send, recv, device):
    return pltpu.make_async_remote_copy(
        src_ref=src,
        dst_ref=dst,
        send_sem=send,
        recv_sem=recv,
        device_id={"frame": device},
        device_id_type=MESH,
    )


def split_heads(low, rows):
    zero = jnp.zeros_like(rows)
    return jnp.concatenate([jnp.where(low, rows, zero), jnp.where(low, zero, rows)], axis=0)


def kernel(
    ndev,
    x_hbm,
    ref_hbm,
    wq_hbm,
    wk_hbm,
    wv_hbm,
    wo_hbm,
    wc_hbm,
    tq_hbm,
    tk_hbm,
    tv_hbm,
    to_hbm,
    out_ref,
    xbuf,
    wqkv,
    wo,
    wc,
    tqkv,
    to,
    refbuf,
    qbuf,
    kbuf,
    vbuf,
    ebuf,
    pbuf,
    abuf,
    fbuf,
    rbuf,
    tab,
    resbuf,
    x_sem,
    w_sem,
    own_sem,
    up_send,
    down_send,
    side_send,
    ref_recv,
    there_send,
    there_recv,
    back_send,
    back_recv,
):
    group, width = xbuf.shape[1:]
    pixels = ndev * group
    pairs = HEADS // 2
    head_dim = width // HEADS
    qscale = LOG2E / math.sqrt(head_dim)
    chunks = fbuf.shape[0]
    size = group // chunks
    block = ndev * size
    line = ndev // 2
    me = lax.axis_index("frame")
    side = lax.rem(me, 2)
    place = me // 2
    partner = me + 1 - 2 * side

    barrier = pltpu.get_barrier_semaphore()

    def greet(device):
        pl.semaphore_signal(barrier, inc=1, device_id={"frame": device}, device_id_type=MESH)

    greet(partner)

    @pl.when(place > 0)
    def _():
        greet(me - 2)

    @pl.when(place < line - 1)
    def _():
        greet(me + 2)

    def columns(index):
        return pl.ds(index * width, width)

    steps = ndev // 2
    own_load = pltpu.make_async_copy(ref_hbm, refbuf.at[me], own_sem)
    x_loads = [
        pltpu.make_async_copy(
            x_hbm.at[pl.ds(2 * step, 2)], xbuf.at[pl.ds(2 * step, 2)], x_sem.at[step]
        )
        for step in range(steps)
    ]
    places = [
        (wq_hbm, wqkv.at[:, columns(0)]),
        (wk_hbm, wqkv.at[:, columns(1)]),
        (wv_hbm, wqkv.at[:, columns(2)]),
        (wo_hbm, wo),
        (wc_hbm, wc),
        (tq_hbm, tqkv.at[:, columns(0)]),
        (tk_hbm, tqkv.at[:, columns(1)]),
        (tv_hbm, tqkv.at[:, columns(2)]),
        (to_hbm, to),
    ]
    w_loads = [
        pltpu.make_async_copy(src, dst, w_sem.at[index]) for index, (src, dst) in enumerate(places)
    ]
    x_loads[0].start()
    for load in w_loads[:3]:
        load.start()
    inner = jnp.logical_and(place > 0, place < line - 1)

    @pl.when(inner)
    def _():
        pl.semaphore_wait(barrier, 3)

    @pl.when(jnp.logical_not(inner))
    def _():
        pl.semaphore_wait(barrier, 2)


    piece = group // PARTS

    def block_copy(sems, slot, owner, part, device, own=False):
        rows = pl.ds(part * piece, piece)
        return remote(
            ref_hbm.at[rows] if own else refbuf.at[owner, rows],
            refbuf.at[owner, rows],
            sems.at[slot * PARTS + part],
            ref_recv.at[owner * PARTS + part],
            device,
        )

    def up_copy(owner, step, part):
        return block_copy(up_send, step, owner, part, me + 2, own=step == 0)

    def down_copy(owner, step, part):
        return block_copy(down_send, step, owner, part, me - 2, own=step == 0)

    def side_copy(owner, slot, part):
        return block_copy(side_send, slot, owner, part, partner, own=slot == 0)

    for part in range(PARTS):

        @pl.when(place < line - 1)
        def _():
            up_copy(me, 0, part).start()

        @pl.when(place > 0)
        def _():
            down_copy(me, 0, part).start()

        side_copy(me, 0, part).start()

    own_load.start()
    for load in x_loads[1:]:
        load.start()
    for load in w_loads[3:]:
        load.start()

    def from_below(step, body):
        @pl.when(place - 1 - step >= 0)
        def _():
            body(me - 2 * (step + 1))

    def from_above(step, body):
        @pl.when(place + 1 + step <= line - 1)
        def _():
            body(me + 2 * (step + 1))

    def hand_on(step):
        for part in range(PARTS):

            def lower(owner):
                side_copy(owner, 1 + 2 * step, part).wait_recv()
                if step < line - 2:

                    @pl.when(place < line - 1)
                    def _():
                        up_copy(owner, step + 1, part).start()

                side_copy(owner, 1 + 2 * step, part).start()

            def upper(owner):
                side_copy(owner, 2 + 2 * step, part).wait_recv()
                if step < line - 2:

                    @pl.when(place > 0)
                    def _():
                        down_copy(owner, step + 1, part).start()

                side_copy(owner, 2 + 2 * step, part).start()

            from_below(step, lower)
            from_above(step, upper)

    def own_rows(step):
        x_loads[step].wait()
        rows = pl.ds(step * 2 * group, 2 * group)
        both = pl.ds(step * 2, 2)
        x = xbuf[both].reshape(2 * group, width)
        normed = layer_norm(x.astype(F32)).astype(BF16)
        projected = dot(normed, wqkv[...])
        qbuf[both] = (projected[:, :width] * qscale).astype(BF16).reshape(2, group, width)
        kbuf[rows, :] = projected[:, width : 2 * width].astype(BF16)
        values = projected[:, 2 * width :].astype(BF16)
        for pair in range(pairs):
            vbuf[pair, rows, 0:128] = values[:, pair * 128 : pair * 128 + 128]
            vbuf[pair, rows, 128:256] = jnp.ones((2 * group, 128), BF16)

    def ref_project(owner):
        slot = owner // 2 + line * lax.rem(owner + me, 2)
        rows = pl.ds(pl.multiple_of(pixels + slot * group, group), group)
        projected = dot(refbuf[owner], wqkv[:, width:])
        kbuf[rows, :] = projected[:, :width].astype(BF16)
        values = projected[:, width:].astype(BF16)
        for pair in range(pairs):
            vbuf[pair, rows, 0:128] = values[:, pair * 128 : pair * 128 + 128]
            vbuf[pair, rows, 128:256] = jnp.ones((group, 128), BF16)

    for load in w_loads[:3]:
        load.wait()
    handed = 0
    for step in range(steps):
        own_rows(step)
        if step % 2 == 1 and handed < line - 1:
            hand_on(handed)
            handed += 1
    own_load.wait()
    ref_project(me)

    def project_line(step):
        from_below(step, ref_project)
        from_above(step, ref_project)

    done = 0
    for step in range(handed, line - 1):
        project_line(done)
        done += 1
        hand_on(step)
    for step in range(done, line - 1):
        project_line(step)

    near = pixels + line * group
    low = lax.broadcasted_iota(jnp.int32, (block, 128), 1) < 64

    def pair_queries(chunk_rows, pair):
        lanes = pl.ds(pair * 128, 128)
        return split_heads(low, qbuf[:, chunk_rows, lanes].reshape(block, 128))

    def early():
        for pair in range(pairs):
            scores = dot_nt(pair_queries(pl.ds(0, size), pair), kbuf[:near, pl.ds(pair * 128, 128)])
            peak = jnp.max(scores, axis=-1, keepdims=True)
            expo = jnp.exp2(scores - peak).astype(BF16)
            ebuf[pair] = dot(expo, vbuf[pair, :near])
            pbuf[pair] = jnp.broadcast_to(peak, (2 * block, 128))

    early()

    def beside(owner):
        for part in range(PARTS):
            side_copy(owner, 1, part).wait_recv()
        ref_project(owner)

    beside(partner)
    for step in range(line - 1):
        from_below(step, lambda owner: beside(owner + partner - me))
        from_above(step, lambda owner: beside(owner + partner - me))

    def there_copy(chunk, target, sender):
        return remote(
            fbuf.at[chunk, target],
            rbuf.at[chunk, sender],
            there_send.at[chunk * ndev + target],
            there_recv.at[chunk * ndev + sender],
            target,
        )

    def back_copy(chunk, target, sender):
        return remote(
            resbuf.at[chunk, target],
            out_ref.at[pl.ds(pl.multiple_of(sender * group + chunk * size, size), size)],
            back_send.at[chunk * ndev + target],
            back_recv.at[chunk * ndev + sender],
            target,
        )

    def send_first(chunk, rows):
        x = xbuf[:, rows, :].reshape(block, width).astype(F32)
        first = (x + dot(abuf[...], wo[...])).astype(BF16)
        fbuf[chunk] = first.reshape(ndev, size, width)
        for off in reversed(range(1, ndev)):
            there_copy(chunk, lax.rem(me + off, ndev), me).start()
        rbuf[chunk, me] = fbuf[chunk, me]

    def put_heads(pair, both):
        mixed = both[:, :128] / both[:, 128:]
        abuf[:, pl.ds(pair * 128, 128)] = jnp.where(low, mixed[:block], mixed[block:]).astype(BF16)

    def finish_first():
        rows = pl.ds(0, size)
        for pair in range(pairs):
            scores = dot_nt(pair_queries(rows, pair), kbuf[near:, pl.ds(pair * 128, 128)])
            before = pbuf[pair]
            peak = jnp.maximum(before[:, :1], jnp.max(scores, axis=-1, keepdims=True))
            expo = jnp.exp2(scores - peak).astype(BF16)
            scale = jnp.exp2(before - jnp.broadcast_to(peak, before.shape))
            scale = jnp.concatenate([scale, scale], axis=1)
            put_heads(pair, ebuf[pair] * scale + dot(expo, vbuf[pair, near:]))
        send_first(0, rows)

    def attend(chunk):
        rows = pl.ds(pl.multiple_of(chunk * size, size), size)
        for pair in range(pairs):
            scores = dot_nt(pair_queries(rows, pair), kbuf[:, pl.ds(pair * 128, 128)])
            peak = jnp.max(scores, axis=-1, keepdims=True)
            expo = jnp.exp2(scores - peak).astype(BF16)
            put_heads(pair, dot(expo, vbuf[pair]))
        send_first(chunk, rows)

    same = lax.rem(lax.broadcasted_iota(jnp.int32, (2 * block, block), 0), size) == lax.rem(
        lax.broadcasted_iota(jnp.int32, (2 * block, block), 1), size
    )

    def temporal(chunk):
        for off in range(1, ndev):
            other = lax.rem(me + off, ndev)
            there_copy(chunk, other, other).wait_recv()
        x = rbuf[chunk].reshape(block, width)
        edge = jnp.zeros((size, width), BF16)
        before = jnp.concatenate([edge, x[:-size]], axis=0)
        after = jnp.concatenate([x[size:], edge], axis=0)
        conv = dot(jnp.concatenate([before, x, after], axis=1), wc[...])
        second = (x.astype(F32) + conv).astype(BF16)
        normed = layer_norm(second.astype(F32)).astype(BF16)
        projected = dot(normed, tqkv[...])
        queries = (projected[:, :width] * qscale).astype(BF16)
        keys = projected[:, width : 2 * width].astype(BF16)
        values = projected[:, 2 * width :].astype(BF16)
        ones = jnp.ones((block, 128), BF16)
        for pair in range(pairs):
            lanes = slice(pair * 128, pair * 128 + 128)
            scores = dot_nt(split_heads(low, queries[:, lanes]), keys[:, lanes])
            scores = jnp.where(same, scores, -1e30)
            peak = jnp.max(scores, axis=-1, keepdims=True)
            expo = jnp.exp2(scores - peak).astype(BF16)
            both = dot(expo, jnp.concatenate([values[:, lanes], ones], axis=1))
            mixed = both[:, :128] / both[:, 128:]
            tab[:, lanes] = jnp.where(low, mixed[:block], mixed[block:]).astype(BF16)
        result = second.astype(F32) + dot(tab[...], to[...])
        resbuf[chunk] = result.astype(BF16).reshape(ndev, size, width)
        for off in reversed(range(1, ndev)):
            back_copy(chunk, lax.rem(me + off, ndev), me).start()
        out_ref[pl.ds(pl.multiple_of(me * group + chunk * size, size), size), :] = resbuf[chunk, me]

    for load in w_loads[3:]:
        load.wait()
    finish_first()

    def stage(step, carry):
        @pl.when(step < chunks)
        def _():
            attend(step)

        @pl.when(step >= LAG)
        def _():
            temporal(step - LAG)

        return carry

    lax.fori_loop(1, chunks + LAG, stage, 0)

    for part in range(PARTS):
        side_copy(me, 0, part).wait_send()
        for step in range(line - 1):

            @pl.when(place < line - 1)
            def _():
                if step == 0:
                    up_copy(me, 0, part).wait_send()
                else:
                    from_below(step - 1, lambda owner: up_copy(owner, step, part).wait_send())

            @pl.when(place > 0)
            def _():
                if step == 0:
                    down_copy(me, 0, part).wait_send()
                else:
                    from_above(step - 1, lambda owner: down_copy(owner, step, part).wait_send())

            from_below(step, lambda owner: side_copy(owner, 1 + 2 * step, part).wait_send())
            from_above(step, lambda owner: side_copy(owner, 2 + 2 * step, part).wait_send())

    for chunk in range(chunks):
        for off in range(1, ndev):
            other = lax.rem(me + off, ndev)
            there_copy(chunk, other, me).wait_send()
            back_copy(chunk, other, me).wait_send()
            back_copy(chunk, other, other).wait_recv()


def per_device(
    frames, ref_rows, w_query, w_key, w_value, w_out, w_conv, t_query, t_key, t_value, t_out
):
    fdev, pixels, width = frames.shape
    ndev = lax.axis_size("frame")
    group = pixels // ndev
    pairs = HEADS // 2
    chunks = group // SIZE
    block = ndev * SIZE
    line = ndev // 2
    DMA = pltpu.SemaphoreType.DMA
    out = pl.pallas_call(
        functools.partial(kernel, ndev),
        out_shape=pltpu.VMEM((pixels, width), BF16),
        in_specs=[pl.BlockSpec(memory_space=pl.ANY)] * 11,
        out_specs=pl.BlockSpec(memory_space=pltpu.VMEM),
        scratch_shapes=[
            pltpu.VMEM((ndev, group, width), BF16),
            pltpu.VMEM((width, 3 * width), BF16),
            pltpu.VMEM((width, width), BF16),
            pltpu.VMEM((3 * width, width), BF16),
            pltpu.VMEM((width, 3 * width), BF16),
            pltpu.VMEM((width, width), BF16),
            pltpu.VMEM((ndev, group, width), BF16),
            pltpu.VMEM((ndev, group, width), BF16),
            pltpu.VMEM((2 * pixels, width), BF16),
            pltpu.VMEM((pairs, 2 * pixels, 256), BF16),
            pltpu.VMEM((pairs, 2 * block, 256), F32),
            pltpu.VMEM((pairs, 2 * block, 128), F32),
            pltpu.VMEM((block, width), BF16),
            pltpu.VMEM((chunks, ndev, SIZE, width), BF16),
            pltpu.VMEM((chunks, ndev, SIZE, width), BF16),
            pltpu.VMEM((block, width), BF16),
            pltpu.VMEM((chunks, ndev, SIZE, width), BF16),
            DMA((line,)),
            DMA((9,)),
            DMA,
            DMA((line * PARTS,)),
            DMA((line * PARTS,)),
            DMA((ndev * PARTS,)),
            DMA((ndev * PARTS,)),
            DMA((chunks * ndev,)),
            DMA((chunks * ndev,)),
            DMA((chunks * ndev,)),
            DMA((chunks * ndev,)),
        ],
        compiler_params=pltpu.CompilerParams(
            collective_id=0, has_side_effects=True, vmem_limit_bytes=56 * 1024 * 1024
        ),
    )(
        frames.reshape(ndev, group, width),
        ref_rows,
        w_query,
        w_key,
        w_value,
        w_out,
        w_conv.reshape(3 * width, width),
        t_query,
        t_key,
        t_value,
        t_out,
    )
    return out.reshape(fdev, pixels, width)


def solution(mesh):
    return jax.shard_map(
        per_device,
        mesh=mesh,
        in_specs=(
            P(("video", "frame"), None, None),
            P(("video", "frame"), None),
            P(),
            P(),
            P(),
            P(),
            P(),
            P(),
            P(),
            P(),
            P(),
        ),
        out_specs=P(("video", "frame"), None, None),
        check_vma=False,
    )
```

```python
import functools
import math

import jax
import jax.numpy as jnp
from jax import lax
from jax.experimental import pallas as pl
from jax.experimental.pallas import tpu as pltpu
from jax.sharding import PartitionSpec as P

HEADS = 10
F32 = jnp.float32
BF16 = jnp.bfloat16
LOG2E = math.log2(math.e)
SIZE = 16
LAG = 3
PARTS = 2
MESH = pl.DeviceIdType.MESH


def layer_norm(value):
    mean = jnp.mean(value, axis=-1, keepdims=True)
    centered = value - mean
    var = jnp.mean(centered * centered, axis=-1, keepdims=True)
    return centered * lax.rsqrt(var + 1e-05)


def dot(a, b):
    return jnp.dot(a, b, preferred_element_type=F32)


def dot_nt(a, b):
    return lax.dot_general(a, b, (((1,), (1,)), ((), ())), preferred_element_type=F32)


def remote(src, dst, send, recv, device):
    return pltpu.make_async_remote_copy(
        src_ref=src,
        dst_ref=dst,
        send_sem=send,
        recv_sem=recv,
        device_id={"frame": device},
        device_id_type=MESH,
    )


def split_heads(low, rows):
    zero = jnp.zeros_like(rows)
    return jnp.concatenate([jnp.where(low, rows, zero), jnp.where(low, zero, rows)], axis=0)


def kernel(
    ndev,
    x_hbm,
    ref_hbm,
    wq_hbm,
    wk_hbm,
    wv_hbm,
    wo_hbm,
    wc_hbm,
    tq_hbm,
    tk_hbm,
    tv_hbm,
    to_hbm,
    out_ref,
    xbuf,
    wqkv,
    wo,
    wc,
    tqkv,
    to,
    refbuf,
    qbuf,
    kbuf,
    vbuf,
    ebuf,
    pbuf,
    abuf,
    fbuf,
    rbuf,
    tab,
    resbuf,
    x_sem,
    w_sem,
    own_sem,
    up_send,
    down_send,
    side_send,
    mate_send,
    ref_recv,
    there_send,
    there_recv,
    back_send,
    back_recv,
):
    group, width = xbuf.shape[1:]
    pixels = ndev * group
    pairs = HEADS // 2
    head_dim = width // HEADS
    qscale = LOG2E / math.sqrt(head_dim)
    chunks = fbuf.shape[0]
    size = group // chunks
    block = ndev * size
    line = ndev // 2
    me = lax.axis_index("frame")
    side = lax.rem(me, 2)
    place = me // 2
    partner = me + 1 - 2 * side
    mate = me + 2 - 4 * lax.rem(place, 2)

    barrier = pltpu.get_barrier_semaphore()

    def greet(device):
        pl.semaphore_signal(barrier, inc=1, device_id={"frame": device}, device_id_type=MESH)

    greet(partner)

    @pl.when(place > 0)
    def _():
        greet(me - 2)

    @pl.when(place < line - 1)
    def _():
        greet(me + 2)

    def columns(index):
        return pl.ds(index * width, width)

    steps = ndev // 2
    own_load = pltpu.make_async_copy(ref_hbm, refbuf.at[me], own_sem)
    x_loads = [
        pltpu.make_async_copy(
            x_hbm.at[pl.ds(2 * step, 2)], xbuf.at[pl.ds(2 * step, 2)], x_sem.at[step]
        )
        for step in range(steps)
    ]
    places = [
        (wq_hbm, wqkv.at[:, columns(0)]),
        (wk_hbm, wqkv.at[:, columns(1)]),
        (wv_hbm, wqkv.at[:, columns(2)]),
        (wo_hbm, wo),
        (wc_hbm, wc),
        (tq_hbm, tqkv.at[:, columns(0)]),
        (tk_hbm, tqkv.at[:, columns(1)]),
        (tv_hbm, tqkv.at[:, columns(2)]),
        (to_hbm, to),
    ]
    w_loads = [
        pltpu.make_async_copy(src, dst, w_sem.at[index]) for index, (src, dst) in enumerate(places)
    ]
    x_loads[0].start()
    for load in w_loads[:3]:
        load.start()
    inner = jnp.logical_and(place > 0, place < line - 1)

    @pl.when(inner)
    def _():
        pl.semaphore_wait(barrier, 3)

    @pl.when(jnp.logical_not(inner))
    def _():
        pl.semaphore_wait(barrier, 2)


    piece = group // PARTS

    def block_copy(sems, slot, owner, part, device, own=False):
        rows = pl.ds(part * piece, piece)
        return remote(
            ref_hbm.at[rows] if own else refbuf.at[owner, rows],
            refbuf.at[owner, rows],
            sems.at[slot * PARTS + part],
            ref_recv.at[owner * PARTS + part],
            device,
        )

    def up_copy(owner, step, part):
        return block_copy(up_send, step, owner, part, me + 2, own=step == 0)

    def down_copy(owner, step, part):
        return block_copy(down_send, step, owner, part, me - 2, own=step == 0)

    def side_copy(owner, slot, part):
        return block_copy(side_send, slot, owner, part, partner, own=slot == 0)

    last = PARTS - 1

    def mate_copy(owner):
        return remote(
            refbuf.at[owner, pl.ds(last * piece, piece)],
            refbuf.at[owner, pl.ds(last * piece, piece)],
            mate_send,
            ref_recv.at[owner * PARTS + last],
            mate,
        )

    def unless_mate(step, part, parity, body):
        if step == 0 and part == last:

            @pl.when(lax.rem(place, 2) == parity)
            def _():
                body()

        else:
            body()

    for part in range(PARTS):

        @pl.when(place < line - 1)
        def _():
            up_copy(me, 0, part).start()

        @pl.when(place > 0)
        def _():
            down_copy(me, 0, part).start()

        side_copy(me, 0, part).start()

    own_load.start()
    for load in x_loads[1:]:
        load.start()
    for load in w_loads[3:]:
        load.start()

    def from_below(step, body):
        @pl.when(place - 1 - step >= 0)
        def _():
            body(me - 2 * (step + 1))

    def from_above(step, body):
        @pl.when(place + 1 + step <= line - 1)
        def _():
            body(me + 2 * (step + 1))

    def hand_on(step):
        for part in range(PARTS):

            def lower(owner):
                side_copy(owner, 1 + 2 * step, part).wait_recv()
                if step < line - 2:

                    @pl.when(place < line - 1)
                    def _():
                        up_copy(owner, step + 1, part).start()

                unless_mate(step, part, 0, side_copy(owner, 1 + 2 * step, part).start)

            def upper(owner):
                side_copy(owner, 2 + 2 * step, part).wait_recv()
                if step < line - 2:

                    @pl.when(place > 0)
                    def _():
                        down_copy(owner, step + 1, part).start()

                unless_mate(step, part, 1, side_copy(owner, 2 + 2 * step, part).start)

            from_below(step, lower)
            from_above(step, upper)
        if step == 0:
            mate_copy(partner).wait_recv()
            mate_copy(partner).start()

    def own_rows(step):
        x_loads[step].wait()
        rows = pl.ds(step * 2 * group, 2 * group)
        both = pl.ds(step * 2, 2)
        x = xbuf[both].reshape(2 * group, width)
        normed = layer_norm(x.astype(F32)).astype(BF16)
        projected = dot(normed, wqkv[...])
        qbuf[both] = (projected[:, :width] * qscale).astype(BF16).reshape(2, group, width)
        kbuf[rows, :] = projected[:, width : 2 * width].astype(BF16)
        values = projected[:, 2 * width :].astype(BF16)
        for pair in range(pairs):
            vbuf[pair, rows, 0:128] = values[:, pair * 128 : pair * 128 + 128]
            vbuf[pair, rows, 128:256] = jnp.ones((2 * group, 128), BF16)

    def ref_project(owner):
        slot = owner // 2 + line * lax.rem(owner + me, 2)
        rows = pl.ds(pl.multiple_of(pixels + slot * group, group), group)
        projected = dot(refbuf[owner], wqkv[:, width:])
        kbuf[rows, :] = projected[:, :width].astype(BF16)
        values = projected[:, width:].astype(BF16)
        for pair in range(pairs):
            vbuf[pair, rows, 0:128] = values[:, pair * 128 : pair * 128 + 128]
            vbuf[pair, rows, 128:256] = jnp.ones((group, 128), BF16)

    for load in w_loads[:3]:
        load.wait()
    handed = 0
    for step in range(steps):
        own_rows(step)
        if step % 2 == 1 and handed < line - 1:
            hand_on(handed)
            handed += 1
    own_load.wait()
    ref_project(me)

    def project_line(step):
        from_below(step, ref_project)
        from_above(step, ref_project)

    nears = [pixels]
    low = lax.broadcasted_iota(jnp.int32, (block, 128), 1) < 64

    def pair_queries(chunk_rows, pair):
        lanes = pl.ds(pair * 128, 128)
        return split_heads(low, qbuf[:, chunk_rows, lanes].reshape(block, 128))

    def early(chunk):
        near = nears[chunk]
        rows = pl.ds(chunk * size, size)
        for pair in range(pairs):
            scores = dot_nt(pair_queries(rows, pair), kbuf[:near, pl.ds(pair * 128, 128)])
            peak = jnp.max(scores, axis=-1, keepdims=True)
            expo = jnp.exp2(scores - peak).astype(BF16)
            ebuf[chunk, pair] = dot(expo, vbuf[pair, :near])
            pbuf[chunk, pair] = jnp.broadcast_to(peak, (2 * block, 128))

    done = 0
    for step in range(handed, line - 1):
        project_line(done)
        done += 1
        early(0)
        hand_on(step)
    for step in range(done, line - 1):
        project_line(step)
    def beside(owner, parts=PARTS):
        for part in range(parts):
            side_copy(owner, 1, part).wait_recv()
        ref_project(owner)

    beside(partner, last)
    for step in range(line - 1):
        from_below(step, lambda owner: beside(owner + partner - me))
        from_above(step, lambda owner: beside(owner + partner - me))

    def opposite(off):
        if ndev & (ndev - 1):
            return lax.rem(me + off, ndev)
        other, bit = me, 1
        while bit < ndev:
            if off & bit:
                other = other + bit - 2 * bit * lax.rem(me // bit, 2)
            bit *= 2
        return other

    def there_copy(chunk, target, sender):
        return remote(
            fbuf.at[chunk, target],
            rbuf.at[chunk, sender],
            there_send.at[chunk * ndev + target],
            there_recv.at[chunk * ndev + sender],
            target,
        )

    def back_copy(chunk, target, sender):
        return remote(
            resbuf.at[chunk, target],
            out_ref.at[pl.ds(pl.multiple_of(sender * group + chunk * size, size), size)],
            back_send.at[chunk * ndev + target],
            back_recv.at[chunk * ndev + sender],
            target,
        )

    def send_first(chunk, rows):
        x = xbuf[:, rows, :].reshape(block, width).astype(F32)
        first = (x + dot(abuf[...], wo[...])).astype(BF16)
        fbuf[chunk] = first.reshape(ndev, size, width)
        for off in range(1, ndev):
            there_copy(chunk, opposite(off), me).start()
        rbuf[chunk, me] = fbuf[chunk, me]

    def put_heads(pair, both):
        mixed = both[:, :128] / both[:, 128:]
        abuf[:, pl.ds(pair * 128, 128)] = jnp.where(low, mixed[:block], mixed[block:]).astype(BF16)

    def finish(chunk):
        near = nears[chunk]
        rows = pl.ds(chunk * size, size)
        for pair in range(pairs):
            scores = dot_nt(pair_queries(rows, pair), kbuf[near:, pl.ds(pair * 128, 128)])
            before = pbuf[chunk, pair]
            peak = jnp.maximum(before[:, :1], jnp.max(scores, axis=-1, keepdims=True))
            expo = jnp.exp2(scores - peak).astype(BF16)
            scale = jnp.exp2(before - jnp.broadcast_to(peak, before.shape))
            scale = jnp.concatenate([scale, scale], axis=1)
            put_heads(pair, ebuf[chunk, pair] * scale + dot(expo, vbuf[pair, near:]))
        send_first(chunk, rows)

    def attend(chunk):
        rows = pl.ds(pl.multiple_of(chunk * size, size), size)
        for pair in range(pairs):
            scores = dot_nt(pair_queries(rows, pair), kbuf[:, pl.ds(pair * 128, 128)])
            peak = jnp.max(scores, axis=-1, keepdims=True)
            expo = jnp.exp2(scores - peak).astype(BF16)
            put_heads(pair, dot(expo, vbuf[pair]))
        send_first(chunk, rows)

    same = lax.rem(lax.broadcasted_iota(jnp.int32, (2 * block, block), 0), size) == lax.rem(
        lax.broadcasted_iota(jnp.int32, (2 * block, block), 1), size
    )

    def temporal(chunk):
        for off in range(1, ndev):
            other = lax.rem(me + off, ndev)
            there_copy(chunk, other, other).wait_recv()
        x = rbuf[chunk].reshape(block, width)
        edge = jnp.zeros((size, width), BF16)
        before = jnp.concatenate([edge, x[:-size]], axis=0)
        after = jnp.concatenate([x[size:], edge], axis=0)
        conv = dot(jnp.concatenate([before, x, after], axis=1), wc[...])
        second = (x.astype(F32) + conv).astype(BF16)
        normed = layer_norm(second.astype(F32)).astype(BF16)
        projected = dot(normed, tqkv[...])
        queries = (projected[:, :width] * qscale).astype(BF16)
        keys = projected[:, width : 2 * width].astype(BF16)
        values = projected[:, 2 * width :].astype(BF16)
        ones = jnp.ones((block, 128), BF16)
        for pair in range(pairs):
            lanes = slice(pair * 128, pair * 128 + 128)
            scores = dot_nt(split_heads(low, queries[:, lanes]), keys[:, lanes])
            scores = jnp.where(same, scores, -1e30)
            peak = jnp.max(scores, axis=-1, keepdims=True)
            expo = jnp.exp2(scores - peak).astype(BF16)
            both = dot(expo, jnp.concatenate([values[:, lanes], ones], axis=1))
            mixed = both[:, :128] / both[:, 128:]
            tab[:, lanes] = jnp.where(low, mixed[:block], mixed[block:]).astype(BF16)
        result = second.astype(F32) + dot(tab[...], to[...])
        resbuf[chunk] = result.astype(BF16).reshape(ndev, size, width)
        for off in range(1, ndev):
            back_copy(chunk, opposite(off), me).start()
        out_ref[pl.ds(pl.multiple_of(me * group + chunk * size, size), size), :] = resbuf[chunk, me]

    for load in w_loads[3:]:
        load.wait()
    for chunk in range(len(nears)):
        finish(chunk)

    def stage(step, carry):
        @pl.when(step < chunks)
        def _():
            attend(step)

        @pl.when(step >= LAG)
        def _():
            temporal(step - LAG)

        return carry

    lax.fori_loop(len(nears), chunks + LAG, stage, 0)

    for part in range(PARTS):
        side_copy(me, 0, part).wait_send()
        for step in range(line - 1):

            @pl.when(place < line - 1)
            def _():
                if step == 0:
                    up_copy(me, 0, part).wait_send()
                else:
                    from_below(step - 1, lambda owner: up_copy(owner, step, part).wait_send())

            @pl.when(place > 0)
            def _():
                if step == 0:
                    down_copy(me, 0, part).wait_send()
                else:
                    from_above(step - 1, lambda owner: down_copy(owner, step, part).wait_send())

            from_below(
                step,
                lambda owner: unless_mate(
                    step, part, 0, side_copy(owner, 1 + 2 * step, part).wait_send
                ),
            )
            from_above(
                step,
                lambda owner: unless_mate(
                    step, part, 1, side_copy(owner, 2 + 2 * step, part).wait_send
                ),
            )
    mate_copy(partner).wait_send()

    for chunk in range(chunks):
        for off in range(1, ndev):
            other = lax.rem(me + off, ndev)
            there_copy(chunk, other, me).wait_send()
            back_copy(chunk, other, me).wait_send()
            back_copy(chunk, other, other).wait_recv()


def per_device(
    frames, ref_rows, w_query, w_key, w_value, w_out, w_conv, t_query, t_key, t_value, t_out
):
    fdev, pixels, width = frames.shape
    ndev = lax.axis_size("frame")
    group = pixels // ndev
    pairs = HEADS // 2
    chunks = group // SIZE
    block = ndev * SIZE
    line = ndev // 2
    DMA = pltpu.SemaphoreType.DMA
    out = pl.pallas_call(
        functools.partial(kernel, ndev),
        out_shape=pltpu.VMEM((pixels, width), BF16),
        in_specs=[pl.BlockSpec(memory_space=pl.ANY)] * 11,
        out_specs=pl.BlockSpec(memory_space=pltpu.VMEM),
        scratch_shapes=[
            pltpu.VMEM((ndev, group, width), BF16),
            pltpu.VMEM((width, 3 * width), BF16),
            pltpu.VMEM((width, width), BF16),
            pltpu.VMEM((3 * width, width), BF16),
            pltpu.VMEM((width, 3 * width), BF16),
            pltpu.VMEM((width, width), BF16),
            pltpu.VMEM((ndev, group, width), BF16),
            pltpu.VMEM((ndev, group, width), BF16),
            pltpu.VMEM((2 * pixels, width), BF16),
            pltpu.VMEM((pairs, 2 * pixels, 256), BF16),
            pltpu.VMEM((1, pairs, 2 * block, 256), F32),
            pltpu.VMEM((1, pairs, 2 * block, 128), F32),
            pltpu.VMEM((block, width), BF16),
            pltpu.VMEM((chunks, ndev, SIZE, width), BF16),
            pltpu.VMEM((chunks, ndev, SIZE, width), BF16),
            pltpu.VMEM((block, width), BF16),
            pltpu.VMEM((chunks, ndev, SIZE, width), BF16),
            DMA((line,)),
            DMA((9,)),
            DMA,
            DMA((line * PARTS,)),
            DMA((line * PARTS,)),
            DMA((ndev * PARTS,)),
            DMA,
            DMA((ndev * PARTS,)),
            DMA((chunks * ndev,)),
            DMA((chunks * ndev,)),
            DMA((chunks * ndev,)),
            DMA((chunks * ndev,)),
        ],
        compiler_params=pltpu.CompilerParams(
            collective_id=0, has_side_effects=True, vmem_limit_bytes=56 * 1024 * 1024
        ),
    )(
        frames.reshape(ndev, group, width),
        ref_rows,
        w_query,
        w_key,
        w_value,
        w_out,
        w_conv.reshape(3 * width, width),
        t_query,
        t_key,
        t_value,
        t_out,
    )
    return out.reshape(fdev, pixels, width)


def solution(mesh):
    return jax.shard_map(
        per_device,
        mesh=mesh,
        in_specs=(
            P(("video", "frame"), None, None),
            P(("video", "frame"), None),
            P(),
            P(),
            P(),
            P(),
            P(),
            P(),
            P(),
            P(),
            P(),
        ),
        out_specs=P(("video", "frame"), None, None),
        check_vma=False,
    )
```

```python
import functools
import math

import jax
import jax.numpy as jnp
from jax import lax
from jax.experimental import pallas as pl
from jax.experimental.pallas import tpu as pltpu
from jax.sharding import PartitionSpec as P

HEADS = 10
F32 = jnp.float32
BF16 = jnp.bfloat16
LOG2E = math.log2(math.e)
SIZE = 16
LAG = 3
PARTS = 2
MESH = pl.DeviceIdType.MESH


def layer_norm(value):
    mean = jnp.mean(value, axis=-1, keepdims=True)
    centered = value - mean
    var = jnp.mean(centered * centered, axis=-1, keepdims=True)
    return centered * lax.rsqrt(var + 1e-05)


def dot(a, b):
    return jnp.dot(a, b, preferred_element_type=F32)


def dot_nt(a, b):
    return lax.dot_general(a, b, (((1,), (1,)), ((), ())), preferred_element_type=F32)


def remote(src, dst, send, recv, device):
    return pltpu.make_async_remote_copy(
        src_ref=src,
        dst_ref=dst,
        send_sem=send,
        recv_sem=recv,
        device_id={"frame": device},
        device_id_type=MESH,
    )


def split_heads(low, rows):
    zero = jnp.zeros_like(rows)
    return jnp.concatenate([jnp.where(low, rows, zero), jnp.where(low, zero, rows)], axis=0)


def kernel(
    ndev,
    x_hbm,
    ref_hbm,
    wq_hbm,
    wk_hbm,
    wv_hbm,
    wo_hbm,
    wc_hbm,
    tq_hbm,
    tk_hbm,
    tv_hbm,
    to_hbm,
    out_ref,
    xbuf,
    wqkv,
    wo,
    wc,
    tqkv,
    to,
    refbuf,
    qbuf,
    kbuf,
    vbuf,
    ebuf,
    pbuf,
    abuf,
    fbuf,
    rbuf,
    tab,
    resbuf,
    x_sem,
    w_sem,
    own_sem,
    up_send,
    down_send,
    side_send,
    mate_send,
    ref_recv,
    there_send,
    there_recv,
    back_send,
    back_recv,
):
    group, width = xbuf.shape[1:]
    pixels = ndev * group
    pairs = HEADS // 2
    head_dim = width // HEADS
    qscale = LOG2E / math.sqrt(head_dim)
    chunks = fbuf.shape[0]
    size = group // chunks
    block = ndev * size
    line = ndev // 2
    me = lax.axis_index("frame")
    side = lax.rem(me, 2)
    place = me // 2
    partner = me + 1 - 2 * side
    mate = me + 2 - 4 * lax.rem(place, 2)

    barrier = pltpu.get_barrier_semaphore()

    def greet(device):
        pl.semaphore_signal(barrier, inc=1, device_id={"frame": device}, device_id_type=MESH)

    greet(partner)

    @pl.when(place > 0)
    def _():
        greet(me - 2)

    @pl.when(place < line - 1)
    def _():
        greet(me + 2)

    def columns(index):
        return pl.ds(index * width, width)

    steps = ndev // 2
    own_load = pltpu.make_async_copy(ref_hbm, refbuf.at[me], own_sem)
    x_loads = [
        pltpu.make_async_copy(
            x_hbm.at[pl.ds(2 * step, 2)], xbuf.at[pl.ds(2 * step, 2)], x_sem.at[step]
        )
        for step in range(steps)
    ]
    places = [
        (wq_hbm, wqkv.at[:, columns(0)]),
        (wk_hbm, wqkv.at[:, columns(1)]),
        (wv_hbm, wqkv.at[:, columns(2)]),
        (wo_hbm, wo),
        (wc_hbm, wc),
        (tq_hbm, tqkv.at[:, columns(0)]),
        (tk_hbm, tqkv.at[:, columns(1)]),
        (tv_hbm, tqkv.at[:, columns(2)]),
        (to_hbm, to),
    ]
    w_loads = [
        pltpu.make_async_copy(src, dst, w_sem.at[index]) for index, (src, dst) in enumerate(places)
    ]
    x_loads[0].start()
    for load in w_loads[:3]:
        load.start()
    inner = jnp.logical_and(place > 0, place < line - 1)

    @pl.when(inner)
    def _():
        pl.semaphore_wait(barrier, 3)

    @pl.when(jnp.logical_not(inner))
    def _():
        pl.semaphore_wait(barrier, 2)


    piece = group // PARTS

    def block_copy(sems, slot, owner, part, device, own=False):
        rows = pl.ds(part * piece, piece)
        return remote(
            ref_hbm.at[rows] if own else refbuf.at[owner, rows],
            refbuf.at[owner, rows],
            sems.at[slot * PARTS + part],
            ref_recv.at[owner * PARTS + part],
            device,
        )

    def up_copy(owner, step, part):
        return block_copy(up_send, step, owner, part, me + 2, own=step == 0)

    def down_copy(owner, step, part):
        return block_copy(down_send, step, owner, part, me - 2, own=step == 0)

    def side_copy(owner, slot, part):
        return block_copy(side_send, slot, owner, part, partner, own=slot == 0)

    last = PARTS - 1

    def mate_copy(owner):
        return remote(
            refbuf.at[owner, pl.ds(last * piece, piece)],
            refbuf.at[owner, pl.ds(last * piece, piece)],
            mate_send,
            ref_recv.at[owner * PARTS + last],
            mate,
        )

    def unless_mate(step, part, parity, body):
        if step == 0 and part == last:

            @pl.when(lax.rem(place, 2) == parity)
            def _():
                body()

        else:
            body()

    for part in range(PARTS):

        @pl.when(place < line - 1)
        def _():
            up_copy(me, 0, part).start()

        @pl.when(place > 0)
        def _():
            down_copy(me, 0, part).start()

        side_copy(me, 0, part).start()

    own_load.start()
    for load in x_loads[1:]:
        load.start()
    for load in w_loads[3:]:
        load.start()

    def from_below(step, body):
        @pl.when(place - 1 - step >= 0)
        def _():
            body(me - 2 * (step + 1))

    def from_above(step, body):
        @pl.when(place + 1 + step <= line - 1)
        def _():
            body(me + 2 * (step + 1))

    def hand_on(step):
        for part in range(PARTS):

            def lower(owner):
                side_copy(owner, 1 + 2 * step, part).wait_recv()
                if step < line - 2:

                    @pl.when(place < line - 1)
                    def _():
                        up_copy(owner, step + 1, part).start()

                unless_mate(step, part, 0, side_copy(owner, 1 + 2 * step, part).start)

            def upper(owner):
                side_copy(owner, 2 + 2 * step, part).wait_recv()
                if step < line - 2:

                    @pl.when(place > 0)
                    def _():
                        down_copy(owner, step + 1, part).start()

                unless_mate(step, part, 1, side_copy(owner, 2 + 2 * step, part).start)

            from_below(step, lower)
            from_above(step, upper)
        if step == 0:
            mate_copy(partner).wait_recv()
            mate_copy(partner).start()

    def own_rows(step):
        x_loads[step].wait()
        rows = pl.ds(step * 2 * group, 2 * group)
        both = pl.ds(step * 2, 2)
        x = xbuf[both].reshape(2 * group, width)
        normed = layer_norm(x.astype(F32)).astype(BF16)
        projected = dot(normed, wqkv[...])
        qbuf[both] = (projected[:, :width] * qscale).astype(BF16).reshape(2, group, width)
        kbuf[rows, :] = projected[:, width : 2 * width].astype(BF16)
        values = projected[:, 2 * width :].astype(BF16)
        for pair in range(pairs):
            vbuf[pair, rows, 0:128] = values[:, pair * 128 : pair * 128 + 128]

    def ref_project(owner):
        slot = owner // 2 + line * lax.rem(owner + me, 2)
        rows = pl.ds(pl.multiple_of(pixels + slot * group, group), group)
        projected = dot(refbuf[owner], wqkv[:, width:])
        kbuf[rows, :] = projected[:, :width].astype(BF16)
        values = projected[:, width:].astype(BF16)
        for pair in range(pairs):
            vbuf[pair, rows, 0:128] = values[:, pair * 128 : pair * 128 + 128]

    vbuf[:, :, 128:256] = jnp.ones((pairs, 2 * pixels, 128), BF16)
    for load in w_loads[:3]:
        load.wait()
    handed = 0
    for step in range(steps):
        own_rows(step)
        if step % 2 == 1 and handed < line - 1:
            hand_on(handed)
            handed += 1
    own_load.wait()
    ref_project(me)

    def project_line(step):
        from_below(step, ref_project)
        from_above(step, ref_project)

    nears = [pixels]
    low = lax.broadcasted_iota(jnp.int32, (block, 128), 1) < 64

    def pair_queries(chunk_rows, pair):
        lanes = pl.ds(pair * 128, 128)
        return split_heads(low, qbuf[:, chunk_rows, lanes].reshape(block, 128))

    def early(chunk):
        near = nears[chunk]
        rows = pl.ds(chunk * size, size)
        for pair in range(pairs):
            scores = dot_nt(pair_queries(rows, pair), kbuf[:near, pl.ds(pair * 128, 128)])
            peak = jnp.max(scores, axis=-1, keepdims=True)
            expo = jnp.exp2(scores - peak).astype(BF16)
            ebuf[chunk, pair] = dot(expo, vbuf[pair, :near])
            pbuf[chunk, pair] = jnp.broadcast_to(peak, (2 * block, 128))

    def beside(owner, parts=PARTS):
        for part in range(parts):
            side_copy(owner, 1, part).wait_recv()
        ref_project(owner)

    done = 0
    for step in range(handed, line - 1):
        project_line(done)
        done += 1
        beside(partner, last)
        early(0)
        hand_on(step)
    for step in range(done, line - 1):
        project_line(step)
    for step in range(line - 1):
        from_below(step, lambda owner: beside(owner + partner - me))
        from_above(step, lambda owner: beside(owner + partner - me))

    def opposite(off):
        if ndev & (ndev - 1):
            return lax.rem(me + off, ndev)
        other, bit = me, 1
        while bit < ndev:
            if off & bit:
                other = other + bit - 2 * bit * lax.rem(me // bit, 2)
            bit *= 2
        return other

    def there_copy(chunk, target, sender):
        return remote(
            fbuf.at[chunk, target],
            rbuf.at[chunk, sender],
            there_send.at[chunk * ndev + target],
            there_recv.at[chunk * ndev + sender],
            target,
        )

    def back_copy(chunk, target, sender):
        return remote(
            resbuf.at[chunk, target],
            out_ref.at[pl.ds(pl.multiple_of(sender * group + chunk * size, size), size)],
            back_send.at[chunk * ndev + target],
            back_recv.at[chunk * ndev + sender],
            target,
        )

    def send_first(chunk, rows):
        x = xbuf[:, rows, :].reshape(block, width).astype(F32)
        first = (x + dot(abuf[...], wo[...])).astype(BF16)
        fbuf[chunk] = first.reshape(ndev, size, width)
        for off in range(1, ndev):
            there_copy(chunk, opposite(off), me).start()
        rbuf[chunk, me] = fbuf[chunk, me]

    def put_heads(pair, both):
        mixed = both[:, :128] / both[:, 128:]
        abuf[:, pl.ds(pair * 128, 128)] = jnp.where(low, mixed[:block], mixed[block:]).astype(BF16)

    def finish(chunk):
        near = nears[chunk]
        rows = pl.ds(chunk * size, size)
        for pair in range(pairs):
            scores = dot_nt(pair_queries(rows, pair), kbuf[near:, pl.ds(pair * 128, 128)])
            before = pbuf[chunk, pair]
            peak = jnp.maximum(before[:, :1], jnp.max(scores, axis=-1, keepdims=True))
            expo = jnp.exp2(scores - peak).astype(BF16)
            scale = jnp.exp2(before - jnp.broadcast_to(peak, before.shape))
            scale = jnp.concatenate([scale, scale], axis=1)
            put_heads(pair, ebuf[chunk, pair] * scale + dot(expo, vbuf[pair, near:]))
        send_first(chunk, rows)

    def attend(chunk):
        rows = pl.ds(pl.multiple_of(chunk * size, size), size)
        for pair in range(pairs):
            scores = dot_nt(pair_queries(rows, pair), kbuf[:, pl.ds(pair * 128, 128)])
            peak = jnp.max(scores, axis=-1, keepdims=True)
            expo = jnp.exp2(scores - peak).astype(BF16)
            put_heads(pair, dot(expo, vbuf[pair]))
        send_first(chunk, rows)

    same = lax.rem(lax.broadcasted_iota(jnp.int32, (2 * block, block), 0), size) == lax.rem(
        lax.broadcasted_iota(jnp.int32, (2 * block, block), 1), size
    )

    def temporal(chunk):
        for off in range(1, ndev):
            other = lax.rem(me + off, ndev)
            there_copy(chunk, other, other).wait_recv()
        x = rbuf[chunk].reshape(block, width)
        edge = jnp.zeros((size, width), BF16)
        before = jnp.concatenate([edge, x[:-size]], axis=0)
        after = jnp.concatenate([x[size:], edge], axis=0)
        conv = dot(jnp.concatenate([before, x, after], axis=1), wc[...])
        second = (x.astype(F32) + conv).astype(BF16)
        normed = layer_norm(second.astype(F32)).astype(BF16)
        projected = dot(normed, tqkv[...])
        queries = (projected[:, :width] * qscale).astype(BF16)
        keys = projected[:, width : 2 * width].astype(BF16)
        values = projected[:, 2 * width :].astype(BF16)
        ones = jnp.ones((block, 128), BF16)
        for pair in range(pairs):
            lanes = slice(pair * 128, pair * 128 + 128)
            scores = dot_nt(split_heads(low, queries[:, lanes]), keys[:, lanes])
            scores = jnp.where(same, scores, -1e30)
            peak = jnp.max(scores, axis=-1, keepdims=True)
            expo = jnp.exp2(scores - peak).astype(BF16)
            both = dot(expo, jnp.concatenate([values[:, lanes], ones], axis=1))
            mixed = both[:, :128] / both[:, 128:]
            tab[:, lanes] = jnp.where(low, mixed[:block], mixed[block:]).astype(BF16)
        result = second.astype(F32) + dot(tab[...], to[...])
        resbuf[chunk] = result.astype(BF16).reshape(ndev, size, width)
        for off in range(1, ndev):
            back_copy(chunk, opposite(off), me).start()
        out_ref[pl.ds(pl.multiple_of(me * group + chunk * size, size), size), :] = resbuf[chunk, me]

    for load in w_loads[3:]:
        load.wait()
    for chunk in range(len(nears)):
        finish(chunk)

    def stage(step, carry):
        @pl.when(step < chunks)
        def _():
            attend(step)

        @pl.when(step >= LAG)
        def _():
            temporal(step - LAG)

        return carry

    lax.fori_loop(len(nears), chunks + LAG, stage, 0)

    for part in range(PARTS):
        side_copy(me, 0, part).wait_send()
        for step in range(line - 1):

            @pl.when(place < line - 1)
            def _():
                if step == 0:
                    up_copy(me, 0, part).wait_send()
                else:
                    from_below(step - 1, lambda owner: up_copy(owner, step, part).wait_send())

            @pl.when(place > 0)
            def _():
                if step == 0:
                    down_copy(me, 0, part).wait_send()
                else:
                    from_above(step - 1, lambda owner: down_copy(owner, step, part).wait_send())

            from_below(
                step,
                lambda owner: unless_mate(
                    step, part, 0, side_copy(owner, 1 + 2 * step, part).wait_send
                ),
            )
            from_above(
                step,
                lambda owner: unless_mate(
                    step, part, 1, side_copy(owner, 2 + 2 * step, part).wait_send
                ),
            )
    mate_copy(partner).wait_send()

    for chunk in range(chunks):
        for off in range(1, ndev):
            other = lax.rem(me + off, ndev)
            there_copy(chunk, other, me).wait_send()
            back_copy(chunk, other, me).wait_send()
            back_copy(chunk, other, other).wait_recv()


def per_device(
    frames, ref_rows, w_query, w_key, w_value, w_out, w_conv, t_query, t_key, t_value, t_out
):
    fdev, pixels, width = frames.shape
    ndev = lax.axis_size("frame")
    group = pixels // ndev
    pairs = HEADS // 2
    chunks = group // SIZE
    block = ndev * SIZE
    line = ndev // 2
    DMA = pltpu.SemaphoreType.DMA
    out = pl.pallas_call(
        functools.partial(kernel, ndev),
        out_shape=pltpu.VMEM((pixels, width), BF16),
        in_specs=[pl.BlockSpec(memory_space=pl.ANY)] * 11,
        out_specs=pl.BlockSpec(memory_space=pltpu.VMEM),
        scratch_shapes=[
            pltpu.VMEM((ndev, group, width), BF16),
            pltpu.VMEM((width, 3 * width), BF16),
            pltpu.VMEM((width, width), BF16),
            pltpu.VMEM((3 * width, width), BF16),
            pltpu.VMEM((width, 3 * width), BF16),
            pltpu.VMEM((width, width), BF16),
            pltpu.VMEM((ndev, group, width), BF16),
            pltpu.VMEM((ndev, group, width), BF16),
            pltpu.VMEM((2 * pixels, width), BF16),
            pltpu.VMEM((pairs, 2 * pixels, 256), BF16),
            pltpu.VMEM((1, pairs, 2 * block, 256), F32),
            pltpu.VMEM((1, pairs, 2 * block, 128), F32),
            pltpu.VMEM((block, width), BF16),
            pltpu.VMEM((chunks, ndev, SIZE, width), BF16),
            pltpu.VMEM((chunks, ndev, SIZE, width), BF16),
            pltpu.VMEM((block, width), BF16),
            pltpu.VMEM((chunks, ndev, SIZE, width), BF16),
            DMA((line,)),
            DMA((9,)),
            DMA,
            DMA((line * PARTS,)),
            DMA((line * PARTS,)),
            DMA((ndev * PARTS,)),
            DMA,
            DMA((ndev * PARTS,)),
            DMA((chunks * ndev,)),
            DMA((chunks * ndev,)),
            DMA((chunks * ndev,)),
            DMA((chunks * ndev,)),
        ],
        compiler_params=pltpu.CompilerParams(
            collective_id=0, has_side_effects=True, vmem_limit_bytes=56 * 1024 * 1024
        ),
    )(
        frames.reshape(ndev, group, width),
        ref_rows,
        w_query,
        w_key,
        w_value,
        w_out,
        w_conv.reshape(3 * width, width),
        t_query,
        t_key,
        t_value,
        t_out,
    )
    return out.reshape(fdev, pixels, width)


def solution(mesh):
    return jax.shard_map(
        per_device,
        mesh=mesh,
        in_specs=(
            P(("video", "frame"), None, None),
            P(("video", "frame"), None),
            P(),
            P(),
            P(),
            P(),
            P(),
            P(),
            P(),
            P(),
            P(),
        ),
        out_specs=P(("video", "frame"), None, None),
        check_vma=False,
    )
```
